32 devices in a mesh: ctx: 8 (over z, x), tp: 4 (over y, core).
Axes of the slice: x: 2, y: 2, z: 4, core: 2. Of those that a mesh axis runs over, the one named last changes fastest.
Arguments:
- query_heads: bfloat16 [2048, 32, 128], P('ctx', 'tp'), may hold values from -6 to 6
- key_heads: bfloat16 [2048, 4, 128], P('ctx', 'tp'), may hold values from -6 to 6
- value_heads: bfloat16 [2048, 4, 128], P('ctx', 'tp'), may hold values from -6 to 6
- attn_out: bfloat16 [2048, 32, 128], P('ctx', 'tp'), may hold values from -6 to 6
- log_sum_exp: float32 [2048, 32], P('ctx', 'tp'), as said below
- positions: int32 [2048], P('ctx'), may hold values from 0 to 2047, as said below
- layer_grad: bfloat16 [2048, 8192], P('ctx', 'tp'), may hold values from -6 to 6
- w_out: bfloat16 [4096, 8192], P('tp'), may hold values from -0.0625 to 0.0625
Outputs:
- query_grad: bfloat16 [2048, 32, 128], P('ctx', 'tp')
- key_grad: bfloat16 [2048, 4, 128], P('ctx', 'tp')
- value_grad: bfloat16 [2048, 4, 128], P('ctx', 'tp')
The draws below stay inside these ranges and needn't reach their ends.
Inputs may be any that keep to these rules, and one draw needn't show every extreme that they name: The sequence is cut into 16 blocks of 128 consecutive positions; the 256 rows of each index of ctx are two whole blocks, numbers b and 15 - b, in either order; every position appears once. log_sum_exp[t, h] is the logarithm of the sum of exp(scores[h, t, u]) over all u with positions[u] <= positions[t].
All inputs are finite; a program needn't handle non-finite values.
Results may differ from the reference program's by a relative error of at most 0.0059.
Values may be sent and summed in bfloat16 or wider, within the bound.
No kernel may reach another device: no remote copies, remote signals or barrier semaphores. Data moves between devices by JAX's collectives and lax.ppermute only.
A program may use at most 64 MiB of HBM per device.

```python
import math
import jax
import jax.numpy as jnp
from jax import lax

D = 8192
HD = 128
GROUP = 8
KVH = 4
QH = 32
HALF = 128
TOKENS = 2048


def layout(key):
    block_count = TOKENS // HALF
    pair_count = block_count // 2
    order = jax.random.permutation(jax.random.fold_in(key, 11), pair_count)
    flipped = jax.random.randint(jax.random.fold_in(key, 12), (pair_count,), 0, 2)
    lower_block = order
    upper_block = block_count - 1 - order
    first_block = jnp.where(flipped == 1, upper_block, lower_block)
    second_block = jnp.where(flipped == 1, lower_block, upper_block)
    starts = jnp.stack([first_block, second_block], axis=1) * HALF
    offsets = jnp.arange(HALF, dtype=jnp.int32)
    return (starts[:, :, None] + offsets[None, None, :]).reshape(TOKENS).astype(jnp.int32)


def features(key, salt, heads):
    subkey = jax.random.fold_in(key, salt)
    base = jax.random.normal(subkey, (TOKENS, heads, HD), jnp.float32)
    return jnp.clip(base, -6.0, 6.0).astype(jnp.bfloat16)


def draw_query_heads(key, part):
    return features(key, 21, QH)


def draw_key_heads(key, part):
    return features(key, 22, KVH)


def draw_positions(key, part):
    return layout(key)


def draw_log_sum_exp(key, part):
    queries = features(key, 21, QH).astype(jnp.float32)
    key_rows = features(key, 22, KVH).astype(jnp.float32)
    places = layout(key)
    visible = places[:, None] >= places[None, :]
    score_scale = 1.0 / math.sqrt(HD)

    def one_head(head_index):
        query_rows = lax.dynamic_index_in_dim(queries, head_index, 1, False)
        group_keys = lax.dynamic_index_in_dim(key_rows, head_index // GROUP, 1, False)
        scores = jnp.dot(query_rows, group_keys.T, precision=lax.Precision.HIGHEST) * score_scale
        return jax.nn.logsumexp(jnp.where(visible, scores, -1e+30), axis=1)
    return jnp.transpose(lax.map(one_head, jnp.arange(QH, dtype=jnp.int32))).astype(jnp.float32)


def shard_levels(key, dims, cuts, least, top_value):
    loudness, own = 1.0, jax.random.fold_in(key, 6)
    for dim, parts in cuts:
        heights = jnp.exp(jax.random.uniform(jax.random.fold_in(own, dim), (parts,), jnp.float32, least / len(cuts), top_value / len(cuts)))
        loudness = loudness * jnp.repeat(heights, dims[dim] // parts).reshape([-1 if axis == dim else 1 for axis in range(len(dims))])
    return loudness


def centred(rng, shape, deviation, most, split=(), held_as=jnp.bfloat16):
    array = deviation * jax.random.normal(rng, shape, jnp.float32)
    if split:
        array = array * shard_levels(rng, shape, split, -0.22, 0.18)
    return jnp.clip(array, -most, most).astype(held_as)


def setup_inputs(seed: int = 0) -> dict:
    arg_keys = jax.random.split(jax.random.key(seed), 9)
    query_heads = draw_query_heads(jax.random.fold_in(arg_keys[8], 71), 0)
    key_heads = draw_key_heads(jax.random.fold_in(arg_keys[8], 71), 0)
    value_heads = centred(arg_keys[2], (TOKENS, KVH, HD), 1.0, 6.0, ((0, 8), (1, 4)))
    attn_out = centred(arg_keys[3], (TOKENS, QH, HD), 1.0, 6.0, ((0, 8), (1, 4)))
    log_sum_exp = draw_log_sum_exp(jax.random.fold_in(arg_keys[8], 71), 0)
    positions = draw_positions(jax.random.fold_in(arg_keys[8], 71), 0)
    layer_grad = centred(arg_keys[6], (TOKENS, D), 1.0, 6.0, ((0, 8), (1, 4)))
    w_out = centred(arg_keys[7], (QH * HD, D), D ** -0.5, 0.0625, ((0, 4),))
    return dict(query_heads=query_heads, key_heads=key_heads, value_heads=value_heads, attn_out=attn_out, log_sum_exp=log_sum_exp, positions=positions, layer_grad=layer_grad, w_out=w_out)


def reference(query_heads, key_heads, value_heads, attn_out, log_sum_exp, positions, layer_grad, w_out):
    score_scale = 1.0 / math.sqrt(HD)
    flat_grad = jnp.dot(layer_grad, w_out.T, preferred_element_type=jnp.float32)
    grad_out = flat_grad.astype(jnp.bfloat16).reshape(TOKENS, QH, HD)
    delta = lax.optimization_barrier(jnp.sum(grad_out.astype(jnp.float32) * attn_out.astype(jnp.float32), axis=2))
    visible = positions[:, None] >= positions[None, :]

    def one_head(head_index):
        kv_index = head_index // GROUP
        queries = lax.dynamic_index_in_dim(query_heads, head_index, 1, False)
        grads = lax.dynamic_index_in_dim(grad_out, head_index, 1, False)
        lse_col = lax.dynamic_index_in_dim(log_sum_exp, head_index, 1, False)
        delta_col = lax.dynamic_index_in_dim(delta, head_index, 1, False)
        key_rows = lax.dynamic_index_in_dim(key_heads, kv_index, 1, False)
        value_rows = lax.dynamic_index_in_dim(value_heads, kv_index, 1, False)
        scores = jnp.dot(queries, key_rows.T, preferred_element_type=jnp.float32) * score_scale
        attn_probs = jnp.where(visible, jnp.exp(scores - lse_col[:, None]), 0.0)
        probs_half = attn_probs.astype(jnp.bfloat16)
        prob_grad = jnp.dot(grads, value_rows.T, preferred_element_type=jnp.float32)
        score_grad = (attn_probs * (prob_grad - delta_col[:, None])).astype(jnp.bfloat16)
        query_term = jnp.dot(score_grad, key_rows, preferred_element_type=jnp.float32)
        key_term = jnp.dot(score_grad.T, queries, preferred_element_type=jnp.float32)
        value_term = jnp.dot(probs_half.T, grads, preferred_element_type=jnp.float32)
        return ((query_term * score_scale).astype(jnp.bfloat16), key_term, value_term)
    query_grads, key_terms, value_terms = lax.map(one_head, jnp.arange(QH, dtype=jnp.int32))
    query_grad = jnp.transpose(query_grads, (1, 0, 2))
    key_sum = lax.optimization_barrier(jnp.sum(key_terms.reshape(KVH, GROUP, TOKENS, HD), axis=1))
    value_sum = lax.optimization_barrier(jnp.sum(value_terms.reshape(KVH, GROUP, TOKENS, HD), axis=1))
    key_grad = jnp.transpose((key_sum * score_scale).astype(jnp.bfloat16), (1, 0, 2))
    value_grad = jnp.transpose(value_sum.astype(jnp.bfloat16), (1, 0, 2))
    return (query_grad, key_grad, value_grad)
```

```python
import functools
import math

import jax
import jax.numpy as jnp
from jax import lax
from jax.experimental import pallas as pl
from jax.experimental.pallas import tpu as pltpu
from jax.sharding import PartitionSpec as P


BF16 = jnp.bfloat16
F32 = jnp.float32
NT = (((1,), (1,)), ((), ()))
VMEM = pl.BlockSpec(memory_space=pltpu.VMEM)
ANY = pl.BlockSpec(memory_space=pl.ANY)
SMEM = pl.BlockSpec(memory_space=pltpu.SMEM)


def swap(x, axis, bits):
    size = lax.axis_size(axis)
    return lax.ppermute(x, axis, [(i, i ^ bits) for i in range(size)])


def project_kernel(first, scalars, a_ref, w_ref, *rest):
    if first:
        (acc_ref,) = rest
    else:
        start_ref, acc_ref = rest
    step = pl.program_id(0)
    term = lax.dot_general(a_ref[...], w_ref[...], NT, preferred_element_type=F32)

    @pl.when(step == 0)
    def _():
        acc_ref[...] = term if first else start_ref[...] + term

    @pl.when(step > 0)
    def _():
        acc_ref[...] += term


def project(part, w_out, quarter, start, row_block, name):
    m, depth = part.shape
    n = w_out.shape[0]
    steps = 4
    width = depth // steps
    scalars = jnp.stack([quarter, row_block]).astype(jnp.int32)
    in_specs = [
        pl.BlockSpec((m, width), lambda i, s: (0, i)),
        pl.BlockSpec((n, width), lambda i, s: (0, s[0] * steps + i)),
    ]
    args = [part, w_out]
    if start is not None:
        in_specs.append(pl.BlockSpec((m, n), lambda i, s: (s[1], 0)))
        args.append(start)
    return pl.pallas_call(
        functools.partial(project_kernel, start is None),
        name=name,
        out_shape=jax.ShapeDtypeStruct((m, n), F32),
        grid_spec=pltpu.PrefetchScalarGridSpec(
            num_scalar_prefetch=1,
            grid=(steps,),
            in_specs=in_specs,
            out_specs=pl.BlockSpec((m, n), lambda i, s: (0, 0)),
        ),
        compiler_params=pltpu.CompilerParams(vmem_limit_bytes=24 << 20),
        cost_estimate=pl.CostEstimate(
            flops=2 * m * n * depth, bytes_accessed=2 * n * depth + 8 * m * n, transcendentals=0
        ),
    )(scalars, *args)


def attend_kernel(
    high, slots, half, heads, hd, row_block, q_ref, ao_ref, lse_ref, pos_ref, acc_ref, *rest
):
    kv_refs = rest[:slots]
    rest = rest[slots:]
    if not high:
        (low_in,) = rest[:1]
        rest = rest[1:]
    dq_ref = rest[0]
    out_refs = rest[1 : 1 + slots]
    rest = rest[1 + slots :]
    if high:
        low_out = rest[0]
        rest = rest[1:]
    (k_buf, v_buf, id_buf, q_rows, q_t, do_rows, do_t, lse_row, delta_row, dq_t, grads, sem) = rest
    width = heads * half
    score_scale = 1.0 / math.sqrt(hd)
    log2e = math.log2(math.e)

    copies = []
    for slot in range(slots):
        at = pl.ds(slot * half, half)
        for buf, source in ((k_buf, 0), (v_buf, 1)):
            copies.append((kv_refs[slot].at[pl.ds(source * half, half)], buf.at[0, at]))
            if high:
                copies.append((kv_refs[slot].at[pl.ds((2 + source) * half, half)], buf.at[1, at]))
        copies.append((kv_refs[slot].at[pl.ds(4 * half, 16)], id_buf.at[slot]))
    copies = [pltpu.make_async_copy(a, b, sem.at[i]) for i, (a, b) in enumerate(copies)]
    for copy in copies:
        copy.start()

    for h in range(heads):
        at = pl.ds(h * half, half)
        part = acc_ref[:, pl.ds(h * hd, hd)].astype(BF16)
        do_rows[at, :] = part
        turned = jnp.transpose(part)
        do_t[:, at] = turned
        saved = jnp.transpose(ao_ref[h]).astype(F32)
        delta_row[:, at] = jnp.sum(turned.astype(F32) * saved, axis=0, keepdims=True)
        q_rows[at, :] = q_ref[h]
        q_t[:, at] = jnp.transpose(q_ref[h])
        lse_row[:, at] = lse_ref[pl.ds(h, 1), :] * log2e
    dq_t[...] = jnp.zeros_like(dq_t)
    places = jnp.broadcast_to(pos_ref[...].astype(F32), (half, half))
    visible = jnp.concatenate([places >= jnp.transpose(places)] * 2, axis=1)
    if high:
        grads[...] = jnp.zeros_like(grads)

    for copy in copies:
        copy.wait()

    def tile(keys, values, mask):
        keys_t = jnp.transpose(keys)
        key_term, value_term = None, None
        for c in range(0, width, 2 * half):
            at = pl.ds(c, 2 * half)
            scores = jnp.dot(keys, q_t[:, at], preferred_element_type=F32)
            probs = jnp.exp2(scores * (score_scale * log2e) - lse_row[:, at])
            if mask is not None:
                probs = jnp.where(mask, probs, 0.0)
            prob_grad = jnp.dot(values, do_t[:, at], preferred_element_type=F32)
            score_grad = (probs * (prob_grad - delta_row[:, at])).astype(BF16)
            key_part = jnp.dot(score_grad, q_rows[at, :], preferred_element_type=F32)
            value_part = jnp.dot(probs.astype(BF16), do_rows[at, :], preferred_element_type=F32)
            key_term = key_part if key_term is None else key_term + key_part
            value_term = value_part if value_term is None else value_term + value_part
            dq_t[:, at] += jnp.dot(keys_t, score_grad, preferred_element_type=F32)
        return key_term * score_scale, value_term

    side = 1 if high else 0
    mine = jnp.max(id_buf[0].astype(F32))

    key_term, value_term = tile(k_buf[side, pl.ds(0, half)], v_buf[side, pl.ds(0, half)], visible)
    if high:
        grads[pl.ds(0, half), pl.ds(0, hd)] = key_term
        grads[pl.ds(0, half), pl.ds(hd, hd)] = value_term
    else:
        grads[pl.ds(0, half), pl.ds(0, hd)] = low_in[pl.ds(0, half), pl.ds(0, hd)] + key_term
        grads[pl.ds(0, half), pl.ds(hd, hd)] = low_in[pl.ds(0, half), pl.ds(hd, hd)] + value_term

    @pl.loop(1, slots)
    def _(slot):
        at = pl.ds(pl.multiple_of(slot * half, half), half)
        theirs = jnp.max(id_buf[slot].astype(F32))
        if not high:
            grads[at, :] = low_in[at, :]

        @pl.when((theirs > mine) if high else (theirs < mine))
        def _():
            key_term, value_term = tile(k_buf[side, at], v_buf[side, at], None)
            if high:
                grads[at, pl.ds(0, hd)] = key_term
                grads[at, pl.ds(hd, hd)] = value_term
            else:
                grads[at, pl.ds(0, hd)] += key_term
                grads[at, pl.ds(hd, hd)] += value_term

    for slot in range(slots):
        out_refs[slot][...] = grads[pl.ds(slot * half, half), :].astype(BF16)

    if high:

        @pl.loop(0, slots // 2)
        def _(pair):
            at = pl.ds(pl.multiple_of(pair * 2 * half, 2 * half), 2 * half)
            key_term, value_term = tile(k_buf[0, at], v_buf[0, at], None)
            low_out[at, pl.ds(0, hd)] = key_term
            low_out[at, pl.ds(hd, hd)] = value_term

    for h in range(heads):
        turned = jnp.transpose(dq_t[:, pl.ds(h * half, half)] * score_scale)
        dq_ref[h] = turned.astype(BF16)


def attend(high, q_hm, ao_hm, lse_hm, pos_row, acc, kv_parts, low_in, row_block):
    heads, rows, hd = q_hm.shape
    half = rows // 2
    slots = len(kv_parts)
    width = heads * half
    block = lambda i, s: (0, s[0], 0)
    in_specs = [
        pl.BlockSpec((heads, half, hd), block),
        pl.BlockSpec((heads, half, hd), block),
        pl.BlockSpec((heads, half), lambda i, s: (0, s[0])),
        pl.BlockSpec((1, half), lambda i, s: (0, s[0])),
        pl.BlockSpec((half, heads * hd), lambda i, s: (0, 0)),
    ]
    in_specs += [ANY] * slots
    args = [q_hm, ao_hm, lse_hm, pos_row, acc, *kv_parts]
    whole3 = lambda i, s: (0, 0, 0)
    whole2 = lambda i, s: (0, 0)
    out_shape = [jax.ShapeDtypeStruct((heads, half, hd), BF16)]
    out_specs = [pl.BlockSpec((heads, half, hd), whole3)]
    out_shape += [jax.ShapeDtypeStruct((half, 2 * hd), BF16)] * slots
    out_specs += [pl.BlockSpec((half, 2 * hd), whole2)] * slots
    if high:
        out_shape.append(jax.ShapeDtypeStruct((slots * half, 2 * hd), F32))
        out_specs.append(pl.BlockSpec((slots * half, 2 * hd), whole2))
    else:
        in_specs.append(pl.BlockSpec((slots * half, 2 * hd), whole2))
        args.append(low_in)
    sides = 2 if high else 1
    blocks = slots + slots // 2 if high else slots // 2
    return pl.pallas_call(
        functools.partial(attend_kernel, high, slots, half, heads, hd),
        name="attend_high" if high else "attend_low",
        out_shape=out_shape,
        grid_spec=pltpu.PrefetchScalarGridSpec(
            num_scalar_prefetch=1,
            grid=(1,),
            in_specs=in_specs,
            out_specs=out_specs,
            scratch_shapes=[
                pltpu.VMEM((sides, slots * half, hd), BF16),
                pltpu.VMEM((sides, slots * half, hd), BF16),
                pltpu.VMEM((slots, 16, hd), BF16),
                pltpu.VMEM((width, hd), BF16),
                pltpu.VMEM((hd, width), BF16),
                pltpu.VMEM((width, hd), BF16),
                pltpu.VMEM((hd, width), BF16),
                pltpu.VMEM((1, width), F32),
                pltpu.VMEM((1, width), F32),
                pltpu.VMEM((hd, width), F32),
                pltpu.VMEM((slots * half, 2 * hd), F32),
                pltpu.SemaphoreType.DMA(((2 * sides + 1) * slots,)),
            ],
        ),
        compiler_params=pltpu.CompilerParams(vmem_limit_bytes=60 << 20),
        cost_estimate=pl.CostEstimate(
            flops=20 * blocks * width * half * hd,
            bytes_accessed=4 << 20,
            transcendentals=blocks * width * half,
        ),
    )(row_block.reshape(1), *args)


def finish_kernel(slots, half, hd, starts, *refs):
    low, high = refs[:slots], refs[slots : 2 * slots]
    dk_ref, dv_ref = refs[2 * slots :]
    for which, parts in ((0, low), (1, high)):
        total = parts[0][...].astype(F32)
        for part in parts[1:]:
            total = total + part[...].astype(F32)
        at = pl.ds(pl.multiple_of(starts[which], half), half)
        dk_ref[at, :] = total[:, :hd].astype(BF16)
        dv_ref[at, :] = total[:, hd:].astype(BF16)


def finish(low_parts, high_parts, starts):
    slots = len(low_parts)
    half, both = low_parts[0].shape
    hd = both // 2
    out = jax.ShapeDtypeStruct((2 * half, hd), BF16)
    return pl.pallas_call(
        functools.partial(finish_kernel, slots, half, hd),
        name="finish",
        out_shape=(out, out),
        in_specs=[SMEM] + [VMEM] * (2 * slots),
        out_specs=(VMEM, VMEM),
        compiler_params=pltpu.CompilerParams(vmem_limit_bytes=16 << 20),
    )(starts, *low_parts, *high_parts)


def local(query_heads, key_heads, value_heads, attn_out, log_sum_exp, positions, layer_grad, w_out):
    rows, heads, hd = query_heads.shape
    half = rows // 2
    slots = lax.axis_size("ctx")
    tp_index = lax.axis_index("tp")

    first_block, second_block = positions[0] // half, positions[half] // half
    high_at = jnp.where(first_block > second_block, 0, 1).astype(jnp.int32)
    low_at = 1 - high_at
    low_number = jnp.minimum(first_block, second_block)

    def rows_of(x, which):
        return lax.dynamic_slice_in_dim(x, which * half, half, 0)

    far_high = swap(rows_of(layer_grad, high_at), "tp", 2)
    far_low = swap(rows_of(layer_grad, low_at), "tp", 2)
    near = swap(layer_grad, "tp", 1)

    keys, values = key_heads[:, 0], value_heads[:, 0]
    own = jnp.concatenate(
        [
            rows_of(keys, low_at),
            rows_of(values, low_at),
            rows_of(keys, high_at),
            rows_of(values, high_at),
            jnp.full((16, hd), low_number, F32).astype(BF16),
        ]
    )
    kv_parts = [own] + [None] * (slots - 1)
    for slot in range(2, slots, 2):
        kv_parts[slot] = swap(own, "ctx", slot)
    for slot in range(0, slots, 2):
        kv_parts[slot + 1] = swap(kv_parts[slot], "ctx", 1)

    q_hm = jnp.transpose(query_heads, (1, 0, 2))
    ao_hm = jnp.transpose(attn_out, (1, 0, 2))
    lse_hm = jnp.transpose(log_sum_exp)
    pos_row = positions.reshape(1, rows)

    zero = jnp.int32(0)
    acc = project(layer_grad, w_out, tp_index, None, zero, "project_own")
    acc = project(near, w_out, tp_index ^ 1, acc, zero, "project_near")

    relay_high = swap(far_high, "tp", 1)
    acc_high = project(far_high, w_out, tp_index ^ 2, acc, high_at, "project_far_high")
    acc_high = project(relay_high, w_out, tp_index ^ 3, acc_high, zero, "project_relay_high")
    *outs, low_sums = attend(
        True, q_hm, ao_hm, lse_hm, pos_row, acc_high, kv_parts, None, high_at
    )
    dq_high, high_parts = outs[0], outs[1:]
    high_parts = [x if s == 0 else swap(x, "ctx", s) for s, x in enumerate(high_parts)]

    relay_low = swap(far_low, "tp", 1)
    acc_low = project(far_low, w_out, tp_index ^ 2, acc, low_at, "project_far_low")
    acc_low = project(relay_low, w_out, tp_index ^ 3, acc_low, zero, "project_relay_low")
    dq_low, *low_parts = attend(
        False, q_hm, ao_hm, lse_hm, pos_row, acc_low, kv_parts, low_sums, low_at
    )
    low_parts = [x if s == 0 else swap(x, "ctx", s) for s, x in enumerate(low_parts)]

    key_grad, value_grad = finish(low_parts, high_parts, jnp.stack([low_at, high_at]) * half)
    both = jnp.where(
        high_at == 0,
        jnp.concatenate([dq_high, dq_low], axis=1),
        jnp.concatenate([dq_low, dq_high], axis=1),
    )
    query_grad = jnp.transpose(both, (1, 0, 2))
    return (query_grad, key_grad[:, None, :], value_grad[:, None, :])


def solution(mesh):
    in_specs = (
        P("ctx", "tp", None),
        P("ctx", "tp", None),
        P("ctx", "tp", None),
        P("ctx", "tp", None),
        P("ctx", "tp"),
        P("ctx"),
        P("ctx", "tp"),
        P("tp", None),
    )
    out_specs = (P("ctx", "tp", None), P("ctx", "tp", None), P("ctx", "tp", None))
    return jax.shard_map(local, mesh=mesh, in_specs=in_specs, out_specs=out_specs, check_vma=False)
```

```python
import functools
import math

import jax
import jax.numpy as jnp
from jax import lax
from jax.experimental import pallas as pl
from jax.experimental.pallas import tpu as pltpu
from jax.sharding import PartitionSpec as P


BF16 = jnp.bfloat16
F32 = jnp.float32
NT = (((1,), (1,)), ((), ()))
VMEM = pl.BlockSpec(memory_space=pltpu.VMEM)
HBM = pl.BlockSpec(memory_space=pltpu.HBM)
SMEM = pl.BlockSpec(memory_space=pltpu.SMEM)
MIB = 1 << 20


def swap(x, axis, bits):
    size = lax.axis_size(axis)
    return lax.ppermute(x, axis, [(i, i ^ bits) for i in range(size)])


def call(kernel, out_shape, in_specs, args, scratch=(), limit=16 * MIB, flops=0, size=0, exps=0):
    return pl.pallas_call(
        kernel,
        out_shape=out_shape,
        in_specs=in_specs,
        out_specs=jax.tree.map(lambda _: VMEM, out_shape),
        scratch_shapes=scratch,
        compiler_params=pltpu.CompilerParams(vmem_limit_bytes=limit),
        cost_estimate=pl.CostEstimate(flops=flops, bytes_accessed=size, transcendentals=exps),
    )(*args)


def shape(dims, dtype):
    return jax.ShapeDtypeStruct(dims, dtype)


def starts_of(pos_ref, half):
    high = jnp.where(pos_ref[0] > pos_ref[half], 0, half)
    return pl.multiple_of(high, half), pl.multiple_of(half - high, half)


def block_number(pos_ref, half):
    return lax.div(jnp.minimum(pos_ref[0], pos_ref[half]), jnp.int32(half))


def prep_kernel(half, pos_ref, lg_ref, k_ref, v_ref, high_ref, low_ref, own_ref, sem):
    high, low = starts_of(pos_ref, half)
    pieces = [
        (lg_ref.at[pl.ds(high, half)], high_ref),
        (lg_ref.at[pl.ds(low, half)], low_ref),
        (k_ref.at[pl.ds(low, half)], own_ref.at[pl.ds(0, half)]),
        (v_ref.at[pl.ds(low, half)], own_ref.at[pl.ds(half, half)]),
        (k_ref.at[pl.ds(high, half)], own_ref.at[pl.ds(2 * half, half)]),
        (v_ref.at[pl.ds(high, half)], own_ref.at[pl.ds(3 * half, half)]),
    ]
    copies = [pltpu.make_async_copy(a, b, sem.at[i]) for i, (a, b) in enumerate(pieces)]
    for copy in copies:
        copy.start()
    number = block_number(pos_ref, half).astype(F32)
    own_ref[pl.ds(4 * half, 16), :] = jnp.full((16, own_ref.shape[1]), number, F32).astype(BF16)
    for copy in copies:
        copy.wait()


def near_kernel(half, heads, hd, *refs):
    (pos_ref, tp_ref, w_ref, high_ref, low_ref, near_ref, q_ref, ao_ref, lse_ref) = refs[:9]
    outs = refs[9:19]
    w_buf, a_buf, raw, flat, acc, sem = refs[19:]
    acc_outs = outs[0:2]
    depth = high_ref.shape[1]
    parts = w_buf.shape[0]
    per = parts // 2
    width = depth // per
    high, low = starts_of(pos_ref, half)
    me = tp_ref[0]
    copies = []
    for i in range(parts):
        quarter = me if i < per else me ^ 1
        at = pl.multiple_of(quarter * depth + (i % per) * width, width)
        copies.append(pltpu.make_async_copy(w_ref.at[:, pl.ds(at, width)], w_buf.at[i], sem.at[i]))
    loads = [
        pltpu.make_async_copy(ref, raw.at[i], sem.at[parts + i])
        for i, ref in enumerate((q_ref, ao_ref))
    ]
    for copy in loads + copies:
        copy.start()

    a_buf[0, pl.ds(0, half), :] = high_ref[...]
    a_buf[0, pl.ds(half, half), :] = low_ref[...]
    a_buf[1, pl.ds(0, half), :] = near_ref[pl.ds(high, half), :]
    a_buf[1, pl.ds(half, half), :] = near_ref[pl.ds(low, half), :]

    for copy in loads:
        copy.wait()
    log2e = math.log2(math.e)
    for which, start in ((0, high), (1, low)):
        q_rows, q_t, ao_t, lse_row = outs[2 + 4 * which : 6 + 4 * which]
        first = pl.multiple_of(start * heads, half * heads)
        for source in (0, 1):
            flat[...] = raw[source, pl.ds(first, half * heads), :].astype(F32)
            for h in range(heads):
                at = pl.ds(h * half, half)
                rows = flat[pl.ds(h, half, stride=heads), :]
                if source == 0:
                    rows = rows.astype(BF16)
                    q_rows[at, :] = rows
                    q_t[:, at] = jnp.transpose(rows)
                else:
                    ao_t[:, at] = jnp.transpose(rows)
        for h in range(heads):
            lse_row[:, pl.ds(h * half, half)] = lse_ref[pl.ds(h, 1), pl.ds(start, half)] * log2e

    n = heads * hd
    for i in range(parts):
        copies[i].wait()
        a_part = a_buf[i // per, :, pl.ds((i % per) * width, width)]

        @pl.loop(0, n // 256)
        def _(block):
            at = pl.ds(pl.multiple_of(block * 256, 256), 256)
            term = lax.dot_general(w_buf[i, at, :], a_part, NT, preferred_element_type=F32)
            if i > 0:
                term = acc[at, :] + term
            if i < parts - 1:
                acc[at, :] = term
            else:
                acc_outs[0][at, :] = term[:, :half]
                acc_outs[1][at, :] = term[:, half:]


def far_kernel(load, *refs):
    if load:
        tp_ref, w_ref, acc_ref, part_ref, out_ref, w2_ref, w3_ref, sem = refs
        depth = part_ref.shape[1]
        copies = []
        for i, (ref, bits) in enumerate(((w2_ref, 2), (w3_ref, 3))):
            at = pl.multiple_of((tp_ref[0] ^ bits) * depth, depth)
            copies.append(pltpu.make_async_copy(w_ref.at[:, pl.ds(at, depth)], ref, sem.at[i]))
        for copy in copies:
            copy.start()
        copies[0].wait()
    else:
        acc_ref, part_ref, w2_ref, out_ref = refs

    @pl.loop(0, acc_ref.shape[0] // 256)
    def _(block):
        at = pl.ds(pl.multiple_of(block * 256, 256), 256)
        term = lax.dot_general(w2_ref[at, :], part_ref[...], NT, preferred_element_type=F32)
        out_ref[at, :] = acc_ref[at, :] + term

    if load:
        copies[1].wait()


def attend_kernel(high, slots, half, heads, hd, *refs):
    pos_ref, row_ref, acc_ref, part_ref, w_ref, q_rows, q_t, ao_t, lse_row = refs[:9]
    refs = refs[9:]
    kv_refs, refs = refs[:slots], refs[slots:]
    if high:
        dq_ref, far_ref, close_ref, even_ref, low_ref = refs[:5]
        refs = refs[5:]
    else:
        low_ref, dq_ref, far_ref, close_ref, even_ref = refs[:5]
        refs = refs[5:]
    k_buf, v_buf, do_rows, do_t, delta_row, dq_t, grads, p_buf, s_buf, listed = refs
    width = heads * half
    score_scale = 1.0 / math.sqrt(hd)
    factor = score_scale * math.log2(math.e)
    mine = block_number(pos_ref, half)

    count = jnp.int32(0)
    if high:
        for slot in range(slots):
            listed[slot] = jnp.int32(slot)
        count = jnp.int32(slots)
    for slot in range(1, slots):
        theirs = jnp.max(kv_refs[slot][pl.ds(4 * half, 16), :].astype(F32)).astype(jnp.int32)
        listed[count] = jnp.int32(slots + slot if high else slot)
        count = count + jnp.where((theirs > mine) if high else (theirs < mine), 1, 0)

    for slot in range(slots):
        at = pl.ds(slot * half, half)
        k_buf[at, :] = kv_refs[slot][pl.ds(0, half), :]
        v_buf[at, :] = kv_refs[slot][pl.ds(half, half), :]
        if high:
            at = pl.ds((slots + slot) * half, half)
            k_buf[at, :] = kv_refs[slot][pl.ds(2 * half, half), :]
            v_buf[at, :] = kv_refs[slot][pl.ds(3 * half, half), :]

    @pl.loop(0, heads)
    def _(h):
        at = pl.ds(pl.multiple_of(h * hd, hd), hd)
        to = pl.ds(pl.multiple_of(h * half, half), half)
        term = lax.dot_general(w_ref[at, :], part_ref[...], NT, preferred_element_type=F32)
        turned = (acc_ref[at, :] + term).astype(BF16)
        do_t[:, to] = turned
        do_rows[to, :] = jnp.transpose(turned)
        delta_row[:, to] = jnp.sum(turned.astype(F32) * ao_t[:, to], axis=0, keepdims=True)

    if high:
        grads[pl.ds(slots * half, slots * half), :] = jnp.zeros((slots * half, 2 * hd), F32)
    else:
        grads[...] = low_ref[...]

    def tile(keys, values, mask):
        m = keys.shape[0]
        keys_t = jnp.transpose(keys)
        for c in range(0, width, 2 * half):
            at = pl.ds(c, 2 * half)
            scores = jnp.dot(keys, q_t[:, at], preferred_element_type=F32)
            probs = jnp.exp2(scores * factor - lse_row[:, at])
            if mask is not None:
                probs = jnp.where(mask, probs, 0.0)
            prob_grad = jnp.dot(values, do_t[:, at], preferred_element_type=F32)
            p_buf[pl.ds(0, m), at] = probs.astype(BF16)
            s_buf[pl.ds(0, m), at] = (probs * (prob_grad - delta_row[:, at])).astype(BF16)
        value_term = jnp.dot(p_buf[pl.ds(0, m), :], do_rows[...], preferred_element_type=F32)
        key_term = jnp.dot(s_buf[pl.ds(0, m), :], q_rows[...], preferred_element_type=F32)
        for c in range(0, width, 2 * half):
            at = pl.ds(c, 2 * half)
            term = jnp.dot(keys_t, s_buf[pl.ds(0, m), at], preferred_element_type=F32)
            if mask is None:
                dq_t[:, at] += term
            else:
                dq_t[:, at] = term
        return key_term * score_scale, value_term

    def put(at, key_term, value_term):
        if not high:
            key_term = grads[at, pl.ds(0, hd)] + key_term
            value_term = grads[at, pl.ds(hd, hd)] + value_term
        grads[at, pl.ds(0, hd)] = key_term
        grads[at, pl.ds(hd, hd)] = value_term

    first, _ = starts_of(pos_ref, half)
    if not high:
        first = pl.multiple_of(half - first, half)
    places = jnp.broadcast_to(row_ref[:, pl.ds(first, half)].astype(F32), (half, half))
    visible = jnp.concatenate([places >= jnp.transpose(places)] * 2, axis=1)
    own = pl.ds(slots * half if high else 0, half)
    put(own, *tile(k_buf[own, :], v_buf[own, :], visible))

    def entry(i):
        return pl.ds(pl.multiple_of(listed[i] * half, half), half)

    @pl.loop(0, lax.div(count, jnp.int32(2)))
    def _(pair):
        one, two = entry(2 * pair), entry(2 * pair + 1)
        keys = jnp.concatenate([k_buf[one, :], k_buf[two, :]], axis=0)
        values = jnp.concatenate([v_buf[one, :], v_buf[two, :]], axis=0)
        key_term, value_term = tile(keys, values, None)
        put(one, key_term[:half], value_term[:half])
        put(two, key_term[half:], value_term[half:])

    @pl.when(lax.rem(count, jnp.int32(2)) == 1)
    def _():
        one = entry(count - 1)
        put(one, *tile(k_buf[one, :], v_buf[one, :], None))

    base = slots if high else 0
    for slot in range(slots):
        part = grads[pl.ds((base + slot) * half, half), :]
        place = (slot // 2) % (slots // 4)
        if slot % 2 == 0:
            even_ref[pl.ds(slot // 2 * half, half), :] = part
        else:
            ref = far_ref if slot >= slots // 2 else close_ref
            ref[pl.ds(place * half, half), :] = part.astype(BF16)
    if high:
        low_ref[...] = grads[pl.ds(0, slots * half), :]
    for h in range(heads):
        turned = jnp.transpose(dq_t[:, pl.ds(h * half, half)] * score_scale)
        dq_ref[h] = turned.astype(BF16)


def attend(high, positions, pos_row, acc, part, w3, sides, kv_parts, low_sums):
    slots = len(kv_parts)
    hd, width = sides[1].shape
    half = part.shape[0]
    heads = width // half
    entries = 2 * slots if high else slots
    args = [positions, pos_row, acc, part, w3, *sides, *kv_parts]
    out_shape = [
        shape((heads, half, hd), BF16),
        shape((slots // 4 * half, 2 * hd), BF16),
        shape((slots // 4 * half, 2 * hd), BF16),
        shape((slots // 2 * half, 2 * hd), F32),
    ]
    if high:
        out_shape.append(shape((slots * half, 2 * hd), F32))
    else:
        args.append(low_sums)
    blocks = slots * 3 // 2 if high else slots // 2
    return call(
        functools.partial(attend_kernel, high, slots, half, heads, hd),
        out_shape,
        [SMEM] + [VMEM] * (len(args) - 1),
        args,
        scratch=[
            pltpu.VMEM((entries * half, hd), BF16),
            pltpu.VMEM((entries * half, hd), BF16),
            pltpu.VMEM((width, hd), BF16),
            pltpu.VMEM((hd, width), BF16),
            pltpu.VMEM((1, width), F32),
            pltpu.VMEM((hd, width), F32),
            pltpu.VMEM((entries * half, 2 * hd), F32),
            pltpu.VMEM((2 * half, width), BF16),
            pltpu.VMEM((2 * half, width), BF16),
            pltpu.SMEM((2 * slots,), jnp.int32),
        ],
        limit=8 * MIB + entries * half * 2 * hd * 8,
        flops=20 * blocks * width * half * hd,
        size=4 * MIB,
        exps=blocks * width * half,
    )


def merge_kernel(half, even_ref, got_ref, *outs):
    for i, out in enumerate(outs):
        at = pl.ds(i * half, half)
        out[...] = (even_ref[at, :] + got_ref[at, :].astype(F32)).astype(out.dtype)


def merge(even, got, half, keep):
    n = got.shape[0] // half
    out_shape = [shape((half, got.shape[1]), F32 if keep and i == 0 else BF16) for i in range(n)]
    return call(
        functools.partial(merge_kernel, half),
        out_shape,
        [VMEM] * 2,
        [even, got],
        limit=4 * MIB,
        size=got.size * 8,
    )


def finish_kernel(count, half, hd, pos_ref, *refs):
    low, high = refs[:count], refs[count : 2 * count]
    dk_ref, dv_ref = refs[2 * count :]
    high_at, low_at = starts_of(pos_ref, half)
    for at, parts in ((low_at, low), (high_at, high)):
        total = parts[0][...]
        for part in parts[1:]:
            total = total + part[...].astype(F32)
        dk_ref[pl.ds(at, half), :] = total[:, :hd].astype(BF16)
        dv_ref[pl.ds(at, half), :] = total[:, hd:].astype(BF16)


def local(query_heads, key_heads, value_heads, attn_out, log_sum_exp, positions, layer_grad, w_out):
    rows, heads, hd = query_heads.shape
    half = rows // 2
    slots = lax.axis_size("ctx")
    depth = layer_grad.shape[1]
    n = w_out.shape[0]
    tp_index = lax.axis_index("tp").astype(jnp.int32).reshape(1)
    pos_row = positions.reshape(1, rows)

    near = swap(layer_grad, "tp", 1)
    lg_high, lg_low, own = call(
        functools.partial(prep_kernel, half),
        [
            shape((half, depth), BF16),
            shape((half, depth), BF16),
            shape((4 * half + 16, hd), BF16),
        ],
        [SMEM, HBM, HBM, HBM],
        [positions, layer_grad, key_heads.reshape(rows, hd), value_heads.reshape(rows, hd)],
        scratch=[pltpu.SemaphoreType.DMA((6,))],
        limit=62 * MIB,
        size=MIB,
    )
    far_high = swap(lg_high, "tp", 2)
    far_low = swap(lg_low, "tp", 2)

    kv_parts = [own] + [None] * (slots - 1)
    for slot in range(slots - 2, 0, -2):
        kv_parts[slot] = swap(own, "ctx", slot)
    for slot in range(0, slots, 2):
        kv_parts[slot + 1] = swap(kv_parts[slot], "ctx", 1)

    width = heads * half
    side = [
        shape((width, hd), BF16),
        shape((hd, width), BF16),
        shape((hd, width), F32),
        shape((1, width), F32),
    ]
    acc_high, acc_low, *sides = call(
        functools.partial(near_kernel, half, heads, hd),
        [shape((n, half), F32)] * 2 + side * 2,
        [SMEM, SMEM, HBM, VMEM, VMEM, VMEM, HBM, HBM, VMEM],
        [
            positions,
            tp_index,
            w_out,
            lg_high,
            lg_low,
            near,
            query_heads.reshape(rows * heads, hd),
            attn_out.reshape(rows * heads, hd),
            jnp.transpose(log_sum_exp),
        ],
        scratch=[
            pltpu.VMEM((4, n, depth // 2), BF16),
            pltpu.VMEM((2, rows, depth), BF16),
            pltpu.VMEM((2, rows * heads, hd), BF16),
            pltpu.VMEM((half * heads, hd), F32),
            pltpu.VMEM((n, rows), F32),
            pltpu.SemaphoreType.DMA((6,)),
        ],
        limit=46 * MIB,
        flops=4 * n * rows * depth,
        size=4 * n * depth,
    )
    relay_high = swap(far_high, "tp", 1)
    acc_high, w2, w3 = call(
        functools.partial(far_kernel, True),
        [shape((n, half), F32), shape((n, depth), BF16), shape((n, depth), BF16)],
        [SMEM, HBM, VMEM, VMEM],
        [tp_index, w_out, acc_high, far_high],
        scratch=[pltpu.SemaphoreType.DMA((2,))],
        limit=44 * MIB,
        flops=2 * n * half * depth,
        size=4 * n * depth,
    )
    dq_high, far_part, close_part, even_high, low_sums = attend(
        True, positions, pos_row, acc_high, relay_high, w3, sides[:4], kv_parts, None
    )
    x_far_high = swap(far_part, "ctx", 1)
    x_close_high = swap(close_part, "ctx", 1)

    relay_low = swap(far_low, "tp", 1)
    acc_low = call(
        functools.partial(far_kernel, False),
        shape((n, half), F32),
        [VMEM] * 3,
        [acc_low, far_low, w2],
        limit=4 * MIB,
        flops=2 * n * half * depth,
        size=2 * n * depth,
    )
    dq_low, far_part, close_part, even_low = attend(
        False, positions, pos_row, acc_low, relay_low, w3, sides[4:], kv_parts, low_sums
    )
    x_far_low = swap(far_part, "ctx", 1)
    x_close_low = swap(close_part, "ctx", 1)

    def z_stage(even, x_far, x_close):
        mid = slots // 4 * half
        far_sums = merge(even[mid:], x_far, half, False)
        close_sums = merge(even[:mid], x_close, half, True)
        got = [swap(x, "ctx", slots // 2 + 2 * i) for i, x in enumerate(far_sums)]
        got += [swap(x, "ctx", 2 * i + 2) for i, x in enumerate(close_sums[1:])]
        return [close_sums[0], *got]

    high_parts = z_stage(even_high, x_far_high, x_close_high)
    low_parts = z_stage(even_low, x_far_low, x_close_low)

    out = shape((rows, hd), BF16)
    key_grad, value_grad = call(
        functools.partial(finish_kernel, slots // 2, half, hd),
        [out, out],
        [SMEM] + [VMEM] * slots,
        [positions, *low_parts, *high_parts],
        limit=4 * MIB,
        size=2 * MIB,
    )
    first_high = positions[0] > positions[half]
    query_grad = jnp.concatenate(
        [
            jnp.where(first_high, dq_high, dq_low),
            jnp.where(first_high, dq_low, dq_high),
        ],
        axis=1,
    )
    query_grad = jnp.transpose(query_grad, (1, 0, 2))
    return (query_grad, key_grad[:, None, :], value_grad[:, None, :])


def solution(mesh):
    in_specs = (
        P("ctx", "tp", None),
        P("ctx", "tp", None),
        P("ctx", "tp", None),
        P("ctx", "tp", None),
        P("ctx", "tp"),
        P("ctx"),
        P("ctx", "tp"),
        P("tp", None),
    )
    out_specs = (P("ctx", "tp", None), P("ctx", "tp", None), P("ctx", "tp", None))

    return jax.shard_map(local, mesh=mesh, in_specs=in_specs, out_specs=out_specs, check_vma=False)
```
